32 devices in a mesh: gx: 2 (over x), gy: 1, gz: 16 (over z, y, core).
Axes of the slice: x: 2, y: 2, z: 4, core: 2. Of those that a mesh axis runs over, the one named last changes fastest.
Arguments:
- volume: bfloat16 [32, 64, 8, 256], P(None, 'gx', 'gy', 'gz'), may hold values from -6 to 6
- weight_a: bfloat16 [3, 3, 3, 32, 64], replicated, may hold values from -0.21875 to 0.21875
- bias_a: float32 [64], replicated, may hold values from -3 to 3
- weight_b: bfloat16 [3, 3, 3, 64, 128], replicated, may hold values from -0.15625 to 0.15625
- bias_b: float32 [128], replicated, may hold values from -3 to 3
- cotangent: bfloat16 [128, 32, 4, 128], P(None, ('gx', 'gz'), 'gy'), may hold values from -24 to 24
Outputs:
- features: bfloat16 [128, 32, 4, 128], P(None, ('gx', 'gz'), 'gy')
- grad_input: bfloat16 [32, 64, 8, 256], P(None, 'gx', 'gy', 'gz')
- grad_weight_a: float32 [3, 3, 3, 32, 64], replicated
- grad_bias_a: float32 [64], replicated
- grad_weight_b: float32 [3, 3, 3, 64, 128], replicated
- grad_bias_b: float32 [128], replicated
The draws below stay inside these ranges and needn't reach their ends.
All inputs are finite; a program needn't handle non-finite values.
Results may differ from the reference program's by a relative error of at most 0.012.
Values may be sent and summed in bfloat16 or wider, within the bound.
A program may use at most 128 MiB of HBM per device.

```python
import math
import jax
import jax.numpy as jnp
from jax import lax

C1 = 32
C2 = 64
C3 = 128
NX = 64
NY = 8
NZ = 256


def level_of(key, dims, shards, least, top_value):
    def one(axis_at, blocks):
        steps = jax.random.uniform(jax.random.fold_in(jax.random.fold_in(key, 6), axis_at), (blocks,), jnp.float32, least / len(shards), top_value / len(shards))
        return jnp.repeat(jnp.exp(steps), dims[axis_at] // blocks).reshape((-1,) + (1,) * (len(dims) - axis_at - 1))

    level = one(*shards[0])
    for cut in shards[1:]:
        level = level * one(*cut)
    return level


def centred(own_key, shape, deviation, limit, cuts=(), dtype=jnp.bfloat16):
    entries = deviation * jax.random.normal(own_key, shape, jnp.float32)
    if cuts:
        entries = entries * level_of(own_key, shape, cuts, -0.22, 0.18)
    return jnp.clip(entries, -limit, limit).astype(dtype)


def setup_inputs(seed: int = 0) -> dict:
    seeds = jax.random.split(jax.random.key(seed), 7)
    return {
        "volume": centred(seeds[0], (C1, NX, NY, NZ), 1.0, 6.0, ((1, 2), (3, 16))),
        "weight_a": centred(seeds[1], (3, 3, 3, C1, C2), (27 * C1) ** -0.5, 0.21875),
        "bias_a": centred(seeds[2], (C2,), 0.5, 3.0, (), jnp.float32),
        "weight_b": centred(seeds[3], (3, 3, 3, C2, C3), (27 * C2) ** -0.5, 0.15625),
        "bias_b": centred(seeds[4], (C3,), 0.5, 3.0, (), jnp.float32),
        "cotangent": centred(seeds[5], (C3, NX // 2, NY // 2, NZ // 2), 4.0, 24.0, ((1, 32),)),
    }


def activate(value):
    return value * jax.nn.sigmoid(value)

def slope_of(value):
    sigma = jax.nn.sigmoid(value)
    return sigma + value * sigma * (1.0 - sigma)

def conv_valid(padded, weight):
    result = lax.conv_general_dilated(padded[None], weight, (1, 1, 1), 'VALID', dimension_numbers=('NCDHW', 'DHWIO', 'NCDHW'), preferred_element_type=jnp.float32)
    return result[0]

def flipped(weight):
    return jnp.transpose(weight[::-1, ::-1, ::-1], (0, 1, 2, 4, 3))

def pad_all(field):
    return jnp.pad(field, ((0, 0), (1, 1), (1, 1), (1, 1)))

def average_pool(field):
    shape = field.shape
    split = field.reshape(shape[0], shape[1] // 2, 2, shape[2] // 2, 2, shape[3] // 2, 2)
    return lax.optimization_barrier(jnp.sum(split, axis=(2, 4, 6))) * 0.125

def spread_back(field):
    shape = field.shape
    larger = jnp.broadcast_to(field[:, :, None, :, None, :, None], (shape[0], shape[1], 2, shape[2], 2, shape[3], 2))
    return larger.reshape(shape[0], 2 * shape[1], 2 * shape[2], 2 * shape[3])

def weight_terms(padded, grad):
    width_in = padded.shape[0]
    width_out = grad.shape[0]
    extent = grad.shape[1:]
    flattened = grad.reshape(width_out, extent[0] * extent[1] * extent[2])
    products = []
    for first in range(3):
        for second in range(3):
            for third in range(3):
                window = padded[:, first:first + extent[0], second:second + extent[1], third:third + extent[2]]
                window = window.reshape(width_in, extent[0] * extent[1] * extent[2])
                products.append(lax.dot_general(window, flattened, (((1,), (1,)), ((), ())), preferred_element_type=jnp.float32))
    return jnp.stack(products).reshape(3, 3, 3, width_in, width_out)

def reference(volume, weight_a, bias_a, weight_b, bias_b, cotangent):
    scale_a = 1.0 / math.sqrt(NX * NY * NZ)
    scale_b = 1.0 / math.sqrt(NX * NY * NZ // 8)
    padded_a = pad_all(volume)
    before_a = conv_valid(padded_a, weight_a) + bias_a[:, None, None, None]
    pooled = average_pool(activate(before_a)).astype(jnp.bfloat16)
    padded_b = pad_all(pooled)
    before_b = conv_valid(padded_b, weight_b) + bias_b[:, None, None, None]
    features = activate(before_b).astype(jnp.bfloat16)
    grad_b = (cotangent.astype(jnp.float32) * slope_of(before_b)).astype(jnp.bfloat16)
    grad_weight_b = weight_terms(padded_b, grad_b) * scale_b
    grad_bias_b = lax.optimization_barrier(jnp.sum(grad_b.astype(jnp.float32), axis=(1, 2, 3))) * scale_b
    grad_pooled = conv_valid(pad_all(grad_b), flipped(weight_b)).astype(jnp.bfloat16)
    grad_a = (spread_back(grad_pooled.astype(jnp.float32)) * 0.125 * slope_of(before_a)).astype(jnp.bfloat16)
    grad_weight_a = weight_terms(padded_a, grad_a) * scale_a
    grad_bias_a = lax.optimization_barrier(jnp.sum(grad_a.astype(jnp.float32), axis=(1, 2, 3))) * scale_a
    grad_input = conv_valid(pad_all(grad_a), flipped(weight_a)).astype(jnp.bfloat16)
    return (features, grad_input, grad_weight_a, grad_bias_a, grad_weight_b, grad_bias_b)
```

```python
import functools
import math

import jax
import jax.numpy as jnp
from jax import lax
from jax.experimental import pallas as pl
from jax.experimental.pallas import tpu as pltpu
from jax.sharding import PartitionSpec as P

LINE = ("gx", "gz")
MESH = pl.DeviceIdType.MESH


def shared(block, axis, dim, width):
    count = lax.axis_size(axis)
    if count == 1:
        edge = jnp.zeros_like(lax.slice_in_dim(block, 0, width, axis=dim))
        return edge, edge
    forward = [(i, i + 1) for i in range(count - 1)]
    backward = [(target, source) for source, target in forward]
    last = block.shape[dim]
    low = lax.ppermute(lax.slice_in_dim(block, last - width, last, axis=dim), axis, forward)
    high = lax.ppermute(lax.slice_in_dim(block, 0, width, axis=dim), axis, backward)
    return low, high


def widened(flat, planes, rows, depth):
    low, high = shared(flat, LINE, 1, rows * depth)
    if lax.axis_size("gy") == 1:
        gap = jnp.zeros((flat.shape[0], depth), flat.dtype)
        pieces = [gap, low, gap]
        for plane in range(planes):
            pieces += [gap, flat[:, plane * rows * depth : (plane + 1) * rows * depth], gap]
        return jnp.concatenate(pieces + [gap, high, gap], axis=1)
    whole = jnp.concatenate([low, flat, high], axis=1)
    whole = whole.reshape(flat.shape[0], planes + 2, rows, depth)
    low, high = shared(whole, "gy", 2, 1)
    return jnp.concatenate([low, whole, high], axis=2).reshape(flat.shape[0], -1)


def slope_of(value):
    sigma = jax.nn.sigmoid(value)
    return sigma + value * sigma * (1.0 - sigma)


def put_windows(wide_ref, windows, planes, rows, depth):
    wide = wide_ref[...]
    width, extent = wide.shape
    place = lax.broadcasted_iota(jnp.int32, (width, extent), 1) % depth
    loose = wide.astype(jnp.float32)
    before = jnp.where(place == 0, 0.0, pltpu.roll(loose, 1, 1)).astype(jnp.bfloat16)
    after = jnp.where(place == depth - 1, 0.0, pltpu.roll(loose, extent - 1, 1)).astype(jnp.bfloat16)
    size = rows * depth
    for third, moved in enumerate((before, wide, after)):
        for first in range(3):
            for second in range(3):
                at = (first * 9 + second * 3 + third) * width
                for plane in range(planes):
                    begin = ((plane + first) * (rows + 2) + second) * depth
                    windows[at : at + width, plane * size : (plane + 1) * size] = moved[
                        :, begin : begin + size
                    ]


def dot_rows(left, right):
    return lax.dot_general(
        left, right, (((1,), (1,)), ((), ())), preferred_element_type=jnp.float32
    )


def forward_a_kernel(dims, wide_ref, weight_ref, bias_ref, pool_ref, before_ref, pooled_ref, windows):
    planes, rows, depth = dims
    put_windows(wide_ref, windows, *dims)
    before = jnp.dot(weight_ref[...], windows[...], preferred_element_type=jnp.float32)
    before = before + bias_ref[...]
    before_ref[...] = before
    active = before * jax.nn.sigmoid(before)
    size = rows * depth
    for row in range(rows // 2):
        parts = [
            active[:, plane * size + (2 * row + j) * depth : plane * size + (2 * row + j + 1) * depth]
            for plane in range(planes)
            for j in range(2)
        ]
        summed = sum(parts[1:], parts[0])
        paired = jnp.dot(
            summed, pool_ref[...], precision=lax.Precision.HIGHEST, preferred_element_type=jnp.float32
        )
        pooled_ref[:, row * depth // 2 : (row + 1) * depth // 2] = (paired * 0.125).astype(jnp.bfloat16)


def middle_kernel(dims, wide_ref, weight_ref, bias_ref, cot_ref, feat_ref, grad_ref, wb_ref, bb_ref, windows):
    put_windows(wide_ref, windows, *dims)
    before = jnp.dot(weight_ref[...], windows[...], preferred_element_type=jnp.float32)
    before = before + bias_ref[...]
    feat_ref[...] = (before * jax.nn.sigmoid(before)).astype(jnp.bfloat16)
    grad = (cot_ref[...].astype(jnp.float32) * slope_of(before)).astype(jnp.bfloat16)
    grad_ref[...] = grad
    wb_ref[...] = dot_rows(windows[...], grad)
    bb_ref[...] = dot_rows(jnp.ones((8, grad.shape[1]), jnp.bfloat16), grad)


def backward_b_kernel(dims, fine, wide_ref, weight_ref, before_ref, spread_ref, grad_ref, windows):
    put_windows(wide_ref, windows, *dims)
    pooled = jnp.dot(weight_ref[...], windows[...], preferred_element_type=jnp.float32)
    pooled = pooled.astype(jnp.bfloat16)
    planes, rows, depth = fine
    size = rows * depth
    for row in range(rows // 2):
        part = pooled[:, row * depth // 2 : (row + 1) * depth // 2]
        spread = jnp.dot(part, spread_ref[...], preferred_element_type=jnp.float32) * 0.125
        for plane in range(planes):
            for j in range(2):
                begin = plane * size + (2 * row + j) * depth
                slope = slope_of(before_ref[:, begin : begin + depth])
                grad_ref[:, begin : begin + depth] = (spread * slope).astype(jnp.bfloat16)


def weight_a_kernel(dims, wide_ref, grad_ref, wa_ref, ba_ref, windows):
    put_windows(wide_ref, windows, *dims)
    grad = grad_ref[...]
    wa_ref[...] = dot_rows(windows[...], grad)
    ba_ref[...] = dot_rows(jnp.ones((8, grad.shape[1]), jnp.bfloat16), grad)


def backward_a_kernel(dims, wide_ref, weight_ref, out_ref, windows):
    put_windows(wide_ref, windows, *dims)
    out = jnp.dot(weight_ref[...], windows[...], preferred_element_type=jnp.float32)
    out_ref[...] = out.astype(jnp.bfloat16)


def local_kernel(body, outs, windows, flops, *operands):
    moved = sum(x.size * x.dtype.itemsize for x in operands)
    return pl.pallas_call(
        body,
        out_shape=[jax.ShapeDtypeStruct(shape, dtype) for shape, dtype in outs],
        in_specs=[pl.BlockSpec(memory_space=pltpu.VMEM)] * len(operands),
        out_specs=[pl.BlockSpec(memory_space=pltpu.VMEM)] * len(outs),
        scratch_shapes=[pltpu.VMEM(windows, jnp.bfloat16)],
        compiler_params=pltpu.CompilerParams(vmem_limit_bytes=48 * 2**20),
        cost_estimate=pl.CostEstimate(flops=flops, bytes_accessed=moved, transcendentals=0),
    )(*operands)


def partner_of(axis, bit):
    me = lax.axis_index(axis)
    mine = (me // bit) % 2
    return me + bit * (1 - 2 * mine), mine


def sum_kernel(steps, halvings, rows, scales, wa_ref, ba_ref, wb_ref, bb_ref, *rest):
    out_wa, out_ba, out_wb, out_bb, acc, gathered, *scratch = rest
    half, width = wa_ref.shape[0] // 2, wa_ref.shape[1]
    top = wb_ref.shape[0]
    count = len(steps)
    sends = scratch[:count]
    recvs = scratch[count : 2 * count]
    sem_send, sem_recv = scratch[2 * count :]
    partners = [partner_of(axis, bit) for axis, bit in steps]
    barrier = pltpu.get_barrier_semaphore()
    for (axis, _), (partner, _) in zip(steps, partners):
        pl.semaphore_signal(barrier, inc=1, device_id={axis: partner}, device_id_type=MESH)
    acc[:top] = wb_ref[...]
    acc[top : top + half, :width] = wa_ref[:half]
    acc[top : top + half, width:] = wa_ref[half:]
    acc[top + half :] = jnp.zeros((rows - top - half, 128), jnp.float32)
    acc[top + half : top + half + 8, :width] = ba_ref[...]
    acc[top + half + 8 : top + half + 16] = bb_ref[...]
    pl.semaphore_wait(barrier, count)
    offset = 0
    size = rows
    kept = []
    for at, ((axis, _), (partner, mine)) in enumerate(zip(steps, partners)):
        source = acc
        if at < halvings:
            size = size // 2
            away = pl.multiple_of(offset + (1 - mine) * size, 16)
            offset = pl.multiple_of(offset + mine * size, 16)
        else:
            away = offset
        sends[at][...] = source[pl.ds(away, size)].astype(jnp.bfloat16)
        copy = pltpu.make_async_remote_copy(
            src_ref=sends[at],
            dst_ref=recvs[at],
            send_sem=sem_send.at[at],
            recv_sem=sem_recv.at[at],
            device_id={axis: partner},
            device_id_type=MESH,
        )
        copy.start()
        copy.wait()
        if at < halvings:
            acc[pl.ds(offset, size)] = source[pl.ds(offset, size)] + recvs[at][...].astype(jnp.float32)
            kept.append((offset, size))
        else:
            acc[pl.ds(offset, size)] = sends[at][...].astype(jnp.float32) + recvs[at][...].astype(jnp.float32)
    gathered[pl.ds(offset, size)] = acc[pl.ds(offset, size)].astype(jnp.bfloat16)
    for back in range(halvings):
        at = halvings - 1 - back
        begin, extent = kept[at]
        (axis, _), (partner, _) = steps[at], partners[at]
        here = gathered.at[pl.ds(begin, extent)]
        copy = pltpu.make_async_remote_copy(
            src_ref=here,
            dst_ref=here,
            send_sem=sem_send.at[count + back],
            recv_sem=sem_recv.at[count + back],
            device_id={axis: partner},
            device_id_type=MESH,
        )
        copy.start()
        copy.wait()
    scale_a, scale_b = scales
    total = gathered[...].astype(jnp.float32)
    out_wb[...] = total[:top] * scale_b
    out_wa[:half] = total[top : top + half, :width] * scale_a
    out_wa[half:] = total[top : top + half, width:] * scale_a
    out_ba[...] = total[top + half : top + half + 1, :width] * scale_a
    out_bb[...] = total[top + half + 8 : top + half + 9] * scale_b


def summed_grads(wa, ba, wb, bb, scales):
    used = wb.shape[0] + wa.shape[0] // 2 + 16
    rows = used + -used % 128
    cut = {
        axis: [2**i for i in range(lax.axis_size(axis).bit_length() - 1)] for axis in ("gz", "gx", "gy")
    }
    steps = [("gz", bit) for bit in cut["gz"][:1]]
    steps += [("gx", bit) for bit in cut["gx"]] + [("gy", bit) for bit in cut["gy"]]
    steps += [("gz", bit) for bit in cut["gz"][1:]]
    halvings = 0
    sizes = []
    size = rows
    for _ in steps:
        if len(sizes) == halvings and size % 32 == 0:
            size //= 2
            halvings += 1
        sizes.append(size)
    buffers = [pltpu.VMEM((s, 128), jnp.bfloat16) for s in sizes]
    total = len(steps) + halvings
    shapes = [wa.shape, (1, ba.shape[1]), wb.shape, (1, bb.shape[1])]
    return pl.pallas_call(
        functools.partial(sum_kernel, steps, halvings, rows, scales),
        out_shape=[jax.ShapeDtypeStruct(shape, jnp.float32) for shape in shapes],
        in_specs=[pl.BlockSpec(memory_space=pltpu.VMEM)] * 4,
        out_specs=[pl.BlockSpec(memory_space=pltpu.VMEM)] * 4,
        scratch_shapes=[
            pltpu.VMEM((rows, 128), jnp.float32),
            pltpu.VMEM((rows, 128), jnp.bfloat16),
            *buffers,
            *buffers,
            pltpu.SemaphoreType.DMA((total,)),
            pltpu.SemaphoreType.DMA((total,)),
        ],
        compiler_params=pltpu.CompilerParams(collective_id=0, has_side_effects=True),
    )(wa, ba, wb, bb)


def outward(weight):
    return weight.reshape(-1, weight.shape[-1]).T


def inward(weight):
    taps = weight[::-1, ::-1, ::-1].reshape(27, *weight.shape[3:])
    return jnp.transpose(taps, (1, 0, 2)).reshape(weight.shape[3], -1)


def on_device(volume, weight_a, bias_a, weight_b, bias_b, cotangent):
    f32, bf16 = jnp.float32, jnp.bfloat16
    count = lax.axis_size("gz")
    devices_all = lax.axis_size("gx") * lax.axis_size("gy") * count
    c1, nx, rows, nz = volume.shape
    cells = nx * rows * nz
    scale_a = 1.0 / math.sqrt(cells * devices_all)
    scale_b = 1.0 / math.sqrt(cells * devices_all // 8)
    c2, c3 = weight_b.shape[3:]
    planes, depth = nx // count, nz * count
    fine = (planes, rows, depth)
    coarse = (planes // 2, rows // 2, depth // 2)
    fewer = cells // 8
    pool = (jnp.arange(depth)[:, None] // 2 == jnp.arange(depth // 2)[None]).astype(f32)
    work_a = 2 * 27 * c1 * c2 * cells
    work_b = 2 * 27 * c2 * c3 * fewer

    slab = lax.all_to_all(volume, "gz", split_axis=1, concat_axis=3, tiled=True).reshape(c1, cells)
    wide_a = widened(slab, *fine)
    before_a, pooled = local_kernel(
        functools.partial(forward_a_kernel, fine),
        [((c2, cells), f32), ((c2, fewer), bf16)],
        (27 * c1, cells),
        work_a,
        wide_a,
        outward(weight_a),
        bias_a[:, None],
        pool,
    )
    wide_b = widened(pooled, *coarse)
    features, grad_b, part_wb, part_bb = local_kernel(
        functools.partial(middle_kernel, coarse),
        [((c3, fewer), bf16), ((c3, fewer), bf16), ((27 * c2, c3), f32), ((8, c3), f32)],
        (27 * c2, fewer),
        2 * work_b,
        wide_b,
        outward(weight_b),
        bias_b[:, None],
        cotangent.reshape(c3, fewer),
    )
    (grad_a,) = local_kernel(
        functools.partial(backward_b_kernel, coarse, fine),
        [((c2, cells), bf16)],
        (27 * c3, fewer),
        work_b,
        widened(grad_b, *coarse),
        inward(weight_b),
        before_a,
        pool.T.astype(bf16),
    )
    part_wa, part_ba = local_kernel(
        functools.partial(weight_a_kernel, fine),
        [((27 * c1, c2), f32), ((8, c2), f32)],
        (27 * c1, cells),
        work_a,
        wide_a,
        grad_a,
    )
    (grad_slab,) = local_kernel(
        functools.partial(backward_a_kernel, fine),
        [((c1, cells), bf16)],
        (27 * c2, cells),
        work_a,
        widened(grad_a, *fine),
        inward(weight_a),
    )
    grad_input = lax.all_to_all(
        grad_slab.reshape(c1, planes, rows, depth), "gz", split_axis=3, concat_axis=1, tiled=True
    )
    sum_wa, sum_ba, sum_wb, sum_bb = summed_grads(
        part_wa, part_ba, part_wb, part_bb, (scale_a, scale_b)
    )
    return (
        features.reshape(cotangent.shape),
        grad_input,
        sum_wa.reshape(weight_a.shape),
        sum_ba.reshape(c2),
        sum_wb.reshape(weight_b.shape),
        sum_bb.reshape(c3),
    )


def solution(mesh):
    return jax.shard_map(
        on_device,
        mesh=mesh,
        in_specs=(P(None, "gx", "gy", "gz"), P(), P(), P(), P(), P(None, ("gx", "gz"), "gy", None)),
        out_specs=(
            P(None, ("gx", "gz"), "gy", None),
            P(None, "gx", "gy", "gz"),
            P(),
            P(),
            P(),
            P(),
        ),
        check_vma=False,
    )
```
